256 devices in a mesh: seq: 32 (over x, z), hid: 8 (over y, core).
Axes of the slice: x: 4, y: 4, z: 8, core: 2. Of those that a mesh axis runs over, the one named last changes fastest.
Arguments:
- tokens: bfloat16 [4096, 4096], P('seq', 'hid'), may hold values from -6 to 6
- hidden_grad: bfloat16 [4096, 14336], P('seq', 'hid'), may hold values from -6 to 6
- gate_blocks: bfloat16 [8, 224, 128, 128], P('hid', 'seq'), may hold values from -0.125 to 0.125
- up_blocks: bfloat16 [8, 224, 128, 128], P('hid', 'seq'), may hold values from -0.125 to 0.125
- gate_rows: int32 [8, 224], P('hid'), may hold values from 0 to 31, as said below
- gate_cols: int32 [8, 224], P('hid'), may hold values from 0 to 13
- gate_count: int32 [8], P('hid'), may hold values from 28 to 224, as said below
- up_rows: int32 [8, 224], P('hid'), may hold values from 0 to 31, as said below
- up_cols: int32 [8, 224], P('hid'), may hold values from 0 to 13
- up_count: int32 [8], P('hid'), may hold values from 28 to 224, as said below
Outputs:
- hidden: bfloat16 [4096, 14336], P('seq', 'hid')
- input_grad: bfloat16 [4096, 4096], P('seq', 'hid')
- gate_block_grads: bfloat16 [8, 224, 128, 128], P('hid', 'seq')
- up_block_grads: bfloat16 [8, 224, 128, 128], P('hid', 'seq')
The draws below stay inside these ranges and needn't reach their ends.
Inputs may be any that keep to these rules, and one draw needn't show every extreme that they name: For each panel, the pairs (gate_rows, gate_cols) over all 224 slots are distinct. `gate_count`: slots at or after a panel's count hold no block of the matrix. For each panel, the pairs (up_rows, up_cols) over all 224 slots are distinct. `up_count`: slots at or after a panel's count hold no block of the matrix.
All inputs are finite; a program needn't handle non-finite values.
Results may differ from the reference program's by a relative error of at most 0.018.
Values may be sent and summed in bfloat16 or wider, within the bound.
No kernel may reach another device: no remote copies, remote signals or barrier semaphores. Data moves between devices by JAX's collectives and lax.ppermute only.
A program may use at most 128 MiB of HBM per device.

```python
import math
import jax
import jax.numpy as jnp
from jax import lax

D = 4096
FF = 14336
BS = 128
TOK_DEV = 128
TOKENS = 4096
CAP = 224
N_SEQ = 32
N_HID = 8


def slot_positions(key, salt):
    total_blocks = D // BS * (FF // N_HID // BS)
    panel_keys = jax.random.split(jax.random.fold_in(key, salt), N_HID)

    def one_panel(panel_key):
        return jax.random.permutation(panel_key, total_blocks)[:CAP]
    return jax.vmap(one_panel)(panel_keys).astype(jnp.int32)


def slot_counts(key, salt):
    lowest = CAP // 8
    highest = CAP // 2
    first, second = jax.random.split(jax.random.fold_in(key, salt), 2)
    counts = jax.random.randint(first, (N_HID,), lowest, highest + 1)
    order = jax.random.permutation(second, N_HID)
    counts = jnp.where(order == 0, CAP, counts)
    counts = jnp.where(order == 1, lowest, counts)
    return counts.astype(jnp.int32)


def draw_gate_rows(key, part):
    return (slot_positions(key, 11) // (FF // N_HID // BS)).astype(jnp.int32)


def draw_gate_cols(key, part):
    return (slot_positions(key, 11) % (FF // N_HID // BS)).astype(jnp.int32)


def draw_up_rows(key, part):
    return (slot_positions(key, 12) // (FF // N_HID // BS)).astype(jnp.int32)


def draw_up_cols(key, part):
    return (slot_positions(key, 12) % (FF // N_HID // BS)).astype(jnp.int32)


def draw_gate_count(key, part):
    return slot_counts(key, 21)


def draw_up_count(key, part):
    return slot_counts(key, 22)


def levels(own_key, dims, cuts, low, high):
    loudness, own = 1.0, jax.random.fold_in(own_key, 6)
    for dim, shards_of in cuts:
        heights = jnp.exp(jax.random.uniform(jax.random.fold_in(own, dim), (shards_of,), jnp.float32, low / len(cuts), high / len(cuts)))
        loudness = loudness * jnp.repeat(heights, dims[dim] // shards_of).reshape([-1 if axis == dim else 1 for axis in range(len(dims))])
    return loudness


def centred(own_key, shape, width, bound, cuts=(), dtype=jnp.bfloat16):
    entries = jax.random.normal(own_key, shape, jnp.float32) * width
    if len(cuts) > 0:
        entries = levels(own_key, shape, cuts, -0.22, 0.18) * entries
    return jnp.clip(entries, min=-bound, max=bound).astype(dtype)


def setup_inputs(seed: int = 0) -> dict:
    keys = jax.random.split(jax.random.key(seed), 11)
    return {
        "tokens": centred(keys[0], (TOKENS, D), 1.0, 6.0, ((0, 32), (1, 8))),
        "hidden_grad": centred(keys[1], (TOKENS, FF), 1.0, 6.0, ((0, 32), (1, 8))),
        "gate_blocks": centred(keys[2], (N_HID, CAP, BS, BS), (D // 2) ** -0.5, 0.125, ((0, 8), (1, 32))),
        "up_blocks": centred(keys[3], (N_HID, CAP, BS, BS), (D // 2) ** -0.5, 0.125, ((0, 8), (1, 32))),
        "gate_rows": draw_gate_rows(jax.random.fold_in(keys[10], 71), 0),
        "gate_cols": draw_gate_cols(jax.random.fold_in(keys[10], 71), 0),
        "gate_count": draw_gate_count(jax.random.fold_in(keys[10], 71), 0),
        "up_rows": draw_up_rows(jax.random.fold_in(keys[10], 71), 0),
        "up_cols": draw_up_cols(jax.random.fold_in(keys[10], 71), 0),
        "up_count": draw_up_count(jax.random.fold_in(keys[10], 71), 0),
    }


def placement_table(indices, active, extent):
    return (indices[:, None] == jnp.arange(extent)[None, :]).astype(jnp.float32) * active[:, None]

def reference(tokens, hidden_grad, gate_blocks, up_blocks, gate_rows, gate_cols, gate_count, up_rows, up_cols, up_count):
    row_blocks = D // BS
    panel_width = FF // N_HID
    col_blocks = panel_width // BS
    slot_ids = jnp.arange(CAP)
    scale = 1.0 / math.sqrt(TOKENS)
    highest = lax.Precision.HIGHEST
    token_tiles = tokens.reshape(N_SEQ, TOK_DEV, row_blocks, BS)
    input_total = jnp.zeros((N_SEQ, TOK_DEV, row_blocks, BS), jnp.float32)
    hidden_parts = []
    gate_grads = []
    up_grads = []
    for panel_index in range(N_HID):
        matrices = []
        for blocks, rows, columns, counts in ((gate_blocks, gate_rows, gate_cols, gate_count), (up_blocks, up_rows, up_cols, up_count)):
            active = (slot_ids < counts[panel_index]).astype(jnp.float32)
            matrices.append((blocks[panel_index].astype(jnp.float32), rows[panel_index], columns[panel_index], active, placement_table(columns[panel_index], active, col_blocks), placement_table(rows[panel_index], active, row_blocks)))
        upstream_all = hidden_grad[:, panel_index * panel_width:(panel_index + 1) * panel_width].reshape(N_SEQ, TOK_DEV, col_blocks, BS)

        def group_step(carry, inputs):
            tiles, upstream = inputs
            picked_inputs = []
            preacts = []
            for weights, rows, columns, active, col_table, row_table in matrices:
                picked = jnp.take(tiles, rows, axis=1).astype(jnp.float32)
                products = jnp.einsum('tsk,skn->tsn', picked, weights, precision=highest)
                preacts.append(jnp.einsum('tsn,sc->tcn', products, col_table, precision=highest))
                picked_inputs.append(picked)
            sigma = jax.nn.sigmoid(preacts[0])
            activated = preacts[0] * sigma
            slope = sigma * (1.0 + preacts[0] * (1.0 - sigma))
            hidden_here = (activated * preacts[1]).astype(jnp.bfloat16)
            upstream_wide = upstream.astype(jnp.float32)
            grads = ((upstream_wide * preacts[1] * slope).astype(jnp.bfloat16), (upstream_wide * activated).astype(jnp.bfloat16))
            input_part = jnp.zeros((TOK_DEV, row_blocks, BS), jnp.float32)
            new_carry = []
            for which in range(2):
                weights, rows, columns, active, col_table, row_table = matrices[which]
                picked_grad = jnp.take(grads[which], columns, axis=1).astype(jnp.float32)
                returned = jnp.einsum('tsn,skn->tsk', picked_grad, weights, precision=highest)
                input_part = input_part + jnp.einsum('tsk,sr->trk', returned, row_table, precision=highest)
                block_term = jnp.einsum('tsk,tsn->skn', picked_inputs[which], picked_grad, precision=highest) * active[:, None, None]
                rounded = lax.optimization_barrier(block_term.astype(jnp.bfloat16)).astype(jnp.float32)
                new_carry.append(carry[which] + rounded)
            return ((new_carry[0], new_carry[1]), (hidden_here, input_part.astype(jnp.bfloat16)))
        start_carry = (jnp.zeros((CAP, BS, BS), jnp.float32), jnp.zeros((CAP, BS, BS), jnp.float32))
        sums, outputs = lax.scan(group_step, start_carry, (token_tiles, upstream_all))
        hidden_parts.append(outputs[0].reshape(TOKENS, panel_width))
        input_total = input_total + outputs[1].astype(jnp.float32)
        gate_grads.append((sums[0] * scale).astype(jnp.bfloat16))
        up_grads.append((sums[1] * scale).astype(jnp.bfloat16))
    hidden = jnp.concatenate(hidden_parts, axis=1)
    input_grad = input_total.reshape(TOKENS, D).astype(jnp.bfloat16)
    return (hidden, input_grad, jnp.stack(gate_grads), jnp.stack(up_grads))
```

```python
import math

import jax
import jax.numpy as jnp
from jax import lax
from jax.experimental import pallas as pl
from jax.experimental.pallas import tpu as pltpu
from jax.sharding import Mesh
from jax.sharding import PartitionSpec as P

AXES = ("xh", "xl", "z", "y", "core")
BS = 128
UNROLL = 4


def tile(index):
    return pl.ds(pl.multiple_of(index * BS, BS), BS)


def forward_kernel(sched, counts, which, x_ref, w_ref, own_ref, send_ref, acc_ref):
    width = own_ref.shape[2]
    core = which[0]
    for matrix in range(2):
        acc_ref[...] = jnp.zeros_like(acc_ref)

        def step(trip, carry):
            products = []
            for u in range(UNROLL):
                q = trip * UNROLL + u
                x = x_ref[:, tile(sched[0, matrix, q])]
                w = w_ref[sched[2, matrix, q]]
                products.append(jnp.dot(x, w, preferred_element_type=jnp.float32))
            for u in range(UNROLL):
                col = tile(sched[1, matrix, trip * UNROLL + u])
                acc_ref[:, col] = acc_ref[:, col] + products[u]
            return carry

        lax.fori_loop(0, pl.cdiv(counts[matrix], UNROLL), step, 0)
        own_ref[matrix] = acc_ref[tile(core), :width]
        send_ref[matrix] = acc_ref[tile(1 - core), :width]


def input_kernel(sched, counts, which, own_g_ref, mate_g_ref, w_ref, own_ref, send_ref, acc_ref, g_ref):
    width = own_ref.shape[1]
    core = which[0]
    acc_ref[...] = jnp.zeros_like(acc_ref)
    for matrix in range(2):
        g_ref[tile(core), :] = own_g_ref[matrix]
        g_ref[tile(1 - core), :] = mate_g_ref[matrix]

        def step(trip, carry):
            products = []
            for u in range(UNROLL):
                q = trip * UNROLL + u
                g = g_ref[:, tile(sched[4, matrix, q])]
                w = w_ref[sched[2, matrix, q]]
                products.append(
                    lax.dot_general(g, w, (((1,), (1,)), ((), ())), preferred_element_type=jnp.float32)
                )
            for u in range(UNROLL):
                row = tile(sched[3, matrix, trip * UNROLL + u])
                acc_ref[:, row] = acc_ref[:, row] + products[u]
            return carry

        lax.fori_loop(0, pl.cdiv(counts[matrix], UNROLL), step, 0)
    own_ref[...] = acc_ref[tile(core), :width].astype(own_ref.dtype)
    send_ref[...] = acc_ref[tile(1 - core), :width].astype(send_ref.dtype)


def weight_kernel(sched, counts, which, own_g_ref, mate_g_ref, xt_ref, out_ref, g_ref):
    core = which[0]
    out_ref[...] = jnp.zeros_like(out_ref)
    for matrix in range(2):
        g_ref[tile(core), :] = own_g_ref[matrix]
        g_ref[tile(1 - core), :] = mate_g_ref[matrix]
        live = counts[matrix]

        def step(trip, carry):
            for u in range(UNROLL):
                q = trip * UNROLL + u
                xt = xt_ref[tile(sched[0, matrix, q]), :]
                g = g_ref[:, tile(sched[4, matrix, q])]
                term = jnp.dot(xt, g, preferred_element_type=jnp.float32)
                term = jnp.where(q < live, term, 0.0)
                out_ref[sched[2, matrix, q]] = term.astype(out_ref.dtype)
            return carry

        lax.fori_loop(0, pl.cdiv(live, UNROLL), step, 0)


def call(kernel, out_shape, scratch, scalars, arrays, flops):
    spec = pl.BlockSpec(memory_space=pltpu.VMEM)
    return pl.pallas_call(
        kernel,
        out_shape=out_shape,
        grid_spec=pltpu.PrefetchScalarGridSpec(
            num_scalar_prefetch=len(scalars),
            grid=(),
            in_specs=[spec] * len(arrays),
            out_specs=jax.tree.map(lambda _: spec, out_shape),
            scratch_shapes=scratch,
        ),
        compiler_params=pltpu.CompilerParams(vmem_limit_bytes=56 * 1024 * 1024),
        cost_estimate=pl.CostEstimate(flops=flops, transcendentals=0, bytes_accessed=10_000_000),
    )(*scalars, *arrays)


def on_device(
    tokens,
    hidden_grad,
    gate_blocks,
    up_blocks,
    gate_rows,
    gate_cols,
    gate_count,
    up_rows,
    up_cols,
    up_count,
):
    sizes = {name: lax.axis_size(name) for name in AXES}
    side = lax.axis_index("xh")
    core = lax.axis_index("core")
    home = side == core
    tok_rows = tokens.shape[0]
    per_owner = gate_blocks.shape[1]
    capacity = gate_rows.shape[1]
    width = hidden_grad.shape[1]
    col_blocks = width // BS

    def swap(value):
        return lax.ppermute(value, ("xh", "core"), [(0, 0), (1, 2), (2, 1), (3, 3)])

    def mate(value):
        return lax.ppermute(value, "core", [(0, 1), (1, 0)])

    stored = swap(jnp.concatenate([gate_blocks[0], up_blocks[0]], axis=0))
    blocks = lax.all_gather(stored, ("xl", "z"), axis=0, tiled=True)

    packed = jnp.concatenate(
        [gate_rows[0], up_rows[0], gate_cols[0], up_cols[0], gate_count, up_count]
    )
    packed = jnp.where(home, packed, mate(packed))
    half = capacity // 2
    tables = packed[: 4 * capacity].reshape(2, 2, 2, half)
    tables = lax.dynamic_index_in_dim(tables, core, 2, keepdims=False)
    live = jnp.clip(packed[4 * capacity :] - core * half, 0, half).astype(jnp.int32)
    slot = jnp.arange(half, dtype=jnp.int32)
    used = slot[None, :] < live[:, None]
    place = (slot // per_owner) * (2 * per_owner) + slot % per_owner
    place = jnp.stack([place, place + per_owner])
    row_blocks = sizes["y"] * sizes["core"] * tokens.shape[1] // BS
    sched = jnp.stack(
        [
            tables[0],
            jnp.where(used, tables[1], col_blocks),
            place,
            jnp.where(used, tables[0], row_blocks),
            tables[1],
        ]
    ).astype(jnp.int32)
    which = core.astype(jnp.int32).reshape(1)

    other = lax.ppermute(tokens, "xh", [(0, 1), (1, 0)])
    pair = jnp.concatenate(
        [jnp.where(side == 0, tokens, other), jnp.where(side == 0, other, tokens)], axis=0
    )
    ny = sizes["y"]
    yid = lax.axis_index("y")
    from_y = [pair] + [
        lax.ppermute(pair, "y", [(i, (i + s) % ny) for i in range(ny)]) for s in range(1, ny)
    ]
    from_y = jnp.stack(from_y)
    from_y = jnp.stack(
        [
            lax.dynamic_index_in_dim(from_y, (yid - i) % ny, 0, keepdims=False)
            for i in range(ny)
        ]
    )
    from_mate = mate(from_y)
    by_core = jnp.stack(
        [jnp.where(core == 0, from_y, from_mate), jnp.where(core == 0, from_mate, from_y)], axis=1
    )
    x = by_core.transpose(2, 0, 1, 3).reshape(2 * tok_rows, row_blocks * BS)
    xt = x.T

    scalars = (sched, live, which)
    pre = jax.ShapeDtypeStruct((2, tok_rows, width), jnp.float32)
    flops = half * 2 * 2 * tok_rows * BS * BS * 2
    own, send = call(
        forward_kernel,
        (pre, pre),
        [pltpu.VMEM((2 * tok_rows, width + BS), jnp.float32)],
        scalars,
        (x, blocks),
        flops,
    )
    summed = own + mate(send)
    gate, up = summed[0], summed[1]
    upstream = swap(hidden_grad).astype(jnp.float32)
    sigma = jax.nn.sigmoid(gate)
    activated = gate * sigma
    slope = sigma * (1.0 + gate * (1.0 - sigma))
    hidden = (activated * up).astype(jnp.bfloat16)
    grads = jnp.stack(
        [(upstream * up * slope).astype(jnp.bfloat16), (upstream * activated).astype(jnp.bfloat16)]
    )
    mate_grads = mate(grads)
    hidden = swap(hidden)

    share = jax.ShapeDtypeStruct((tok_rows, row_blocks * BS), jnp.bfloat16)
    own_in, send_in = call(
        input_kernel,
        (share, share),
        [
            pltpu.VMEM((2 * tok_rows, (row_blocks + 1) * BS), jnp.float32),
            pltpu.VMEM((2 * tok_rows, width), jnp.bfloat16),
        ],
        scalars,
        (grads, mate_grads, blocks),
        flops,
    )
    panel_input = (own_in.astype(jnp.float32) + mate(send_in).astype(jnp.float32)).astype(jnp.bfloat16)
    input_grad = swap(lax.psum_scatter(panel_input, ("y", "xh"), scatter_dimension=1, tiled=True))

    terms = call(
        weight_kernel,
        jax.ShapeDtypeStruct(blocks.shape, jnp.bfloat16),
        [pltpu.VMEM((2 * tok_rows, width), jnp.bfloat16)],
        scalars,
        (grads, mate_grads, xt),
        flops,
    )
    terms = lax.psum_scatter(terms, ("xl", "z"), scatter_dimension=0, tiled=True)
    scale = 1.0 / math.sqrt(tok_rows * sizes["xh"] * sizes["xl"] * sizes["z"])
    terms = swap((terms.astype(jnp.float32) * scale).astype(jnp.bfloat16))
    return hidden, input_grad, terms[None, :per_owner], terms[None, per_owner:]


def solution(mesh):
    shape = mesh.devices.shape
    fine = Mesh(mesh.devices.reshape(2, 2, shape[0] // 4, shape[1] // 2, 2), AXES)
    seq, hid = ("xh", "xl", "z"), ("y", "core")
    placed = (
        P(seq, hid),
        P(seq, hid),
        P(hid, seq, None, None),
        P(hid, seq, None, None),
        P(hid, None),
        P(hid, None),
        P(hid),
        P(hid, None),
        P(hid, None),
        P(hid),
    )
    return jax.shard_map(
        on_device,
        mesh=fine,
        in_specs=placed,
        out_specs=(P(seq, hid), P(seq, hid), P(hid, seq, None, None), P(hid, seq, None, None)),
        check_vma=False,
    )
```

```python
import math

import jax
import jax.numpy as jnp
import numpy as np
from jax import lax
from jax.experimental import pallas as pl
from jax.experimental.pallas import tpu as pltpu
from jax.sharding import Mesh
from jax.sharding import PartitionSpec as P

AXES = ("xh", "xl", "z", "y", "core")
BS = 128
VMEM_LIMIT = 56 * 1024 * 1024

GATE_RUNS = [(d, r) for d in range(8) for r in (0, 1)]
UP_RUNS = [(d, r) for r in (0, 1) for d in range(8)]
EARLY_RUNS = 8


def tile(index):
    return pl.ds(pl.multiple_of(index * BS, BS), BS)


def start_copies(copies, block_refs, w_ref, sems):
    started = []
    for number, (which, start, size, target) in enumerate(copies):
        copy = pltpu.make_async_copy(
            block_refs[which].at[pl.ds(start, size)], w_ref.at[pl.ds(target, size)], sems.at[number]
        )
        copy.start()
        started.append(copy)
    return started


def over_runs(copies, started, count, run_first, run, body):
    early = EARLY_RUNS * run
    for piece, copy in zip(copies, started):
        if piece[3] < early:
            copy.wait()

    def visit(index, carry):
        first = run_first(index)

        @pl.when(first < count)
        def _():
            body(index, first)

        return carry

    lax.fori_loop(0, EARLY_RUNS, visit, 0)
    for piece, copy in zip(copies, started):
        if piece[3] >= early:
            copy.wait()
    lax.fori_loop(EARLY_RUNS, len(GATE_RUNS), visit, 0)


class Lists:
    def __init__(self, lists, place, table, matrix, capacity, run, nz):
        self.lists, self.place, self.table = lists, place, table
        self.rows, self.cols = 2 * matrix * capacity, (2 * matrix + 1) * capacity
        self.count = lists[4 * capacity + matrix]
        self.capacity, self.run, self.nz = capacity, run, nz

    def first(self, index):
        z = self.table[0, index]
        xl = self.place[0] ^ self.table[1, index]
        return (((self.place[1] ^ (z % 2)) * 2 + xl) * self.nz + z) * self.run

    def row(self, slot):
        return self.lists[self.rows + slot]

    def col(self, slot):
        return self.lists[self.cols + slot]


def table_of(runs):
    return jnp.asarray(np.asarray(runs, np.int32).T)


def forward_call(scalars, matrix, capacity, nz, x, blocks, copies, width, run):
    tok_rows = x.shape[0] // 2
    slots = len(GATE_RUNS) * run

    def kernel(lists, place, table, x_ref, *refs):
        block_refs = refs[: len(blocks)]
        own_ref, send_ref, acc_ref, w_ref, sems = refs[len(blocks) :]
        known = Lists(lists, place, table, matrix, capacity, run, nz)
        started = start_copies(copies, block_refs, w_ref, sems)
        acc_ref[...] = jnp.zeros_like(acc_ref)

        def body(index, first):
            for part in (range(0, 4), range(4, run)):
                products = []
                for u in part:
                    x = x_ref[:, tile(known.row(first + u))]
                    products.append(jnp.dot(x, w_ref[index * run + u], preferred_element_type=jnp.float32))
                for u, product in zip(part, products):
                    col = jnp.where(first + u < known.count, known.col(first + u), width // BS)
                    acc_ref[:, tile(col)] = acc_ref[:, tile(col)] + product

        over_runs(copies, started, known.count, known.first, run, body)
        half = place[2]
        own_ref[...] = acc_ref[tile(half), :width]
        send_ref[...] = acc_ref[tile(1 - half), :width]

    vmem = pl.BlockSpec(memory_space=pltpu.VMEM)
    out = jax.ShapeDtypeStruct((tok_rows, width), jnp.float32)
    return pl.pallas_call(
        kernel,
        name="forward",
        out_shape=(out, out),
        grid_spec=pltpu.PrefetchScalarGridSpec(
            num_scalar_prefetch=3,
            grid=(),
            in_specs=[vmem] + [pl.BlockSpec(memory_space=pl.ANY)] * len(blocks),
            out_specs=(vmem, vmem),
            scratch_shapes=[
                pltpu.VMEM((2 * tok_rows, width + BS), jnp.float32),
                pltpu.VMEM((slots, BS, BS), jnp.bfloat16),
                pltpu.SemaphoreType.DMA((len(copies),)),
            ],
        ),
        compiler_params=pltpu.CompilerParams(vmem_limit_bytes=VMEM_LIMIT),
        cost_estimate=pl.CostEstimate(
            flops=slots * 4 * tok_rows * BS * BS, transcendentals=0, bytes_accessed=8_000_000
        ),
    )(*scalars, x, *blocks)


def input_call(scalars, matrix, capacity, nz, own_g, mate_g, previous, blocks, copies, shape, run):
    tok_rows = own_g.shape[0]
    width = own_g.shape[1]
    features = shape[0] * shape[1] * shape[3]
    slots = len(GATE_RUNS) * run
    last = previous is not None
    previous = previous if last else ()

    def kernel(lists, place, table, own_g_ref, mate_g_ref, *refs):
        before = refs[: len(previous)]
        block_refs = refs[len(previous) : len(previous) + len(blocks)]
        own_ref, send_ref, acc_ref, g_ref, w_ref, sems = refs[len(previous) + len(blocks) :]
        known = Lists(lists, place, table, matrix, capacity, run, nz)
        started = start_copies(copies, block_refs, w_ref, sems)
        mine, other = tile(place[2]), tile(1 - place[2])
        if last:
            acc_ref[mine, :features] = before[0][...]
            acc_ref[other, :features] = before[1][...]
        else:
            acc_ref[...] = jnp.zeros_like(acc_ref)
        g_ref[mine, :] = own_g_ref[...]
        g_ref[other, :] = mate_g_ref[...]

        def body(index, first):
            for part in (range(0, 4), range(4, run)):
                products = []
                for u in part:
                    g = g_ref[:, tile(known.col(first + u))]
                    products.append(
                        lax.dot_general(
                            g,
                            w_ref[index * run + u],
                            (((1,), (1,)), ((), ())),
                            preferred_element_type=jnp.float32,
                        )
                    )
                for u, product in zip(part, products):
                    row = jnp.where(first + u < known.count, known.row(first + u), features // BS)
                    acc_ref[:, tile(row)] = acc_ref[:, tile(row)] + product

        over_runs(copies, started, known.count, known.first, run, body)
        if last:
            step = shape[3]
            for high in range(shape[0]):
                for y in range(shape[1]):
                    cut = pl.ds((y * shape[0] + high) * step, step)
                    own_ref[high, y] = acc_ref[mine, cut].astype(own_ref.dtype)
                    send_ref[high, y] = acc_ref[other, cut].astype(send_ref.dtype)
        else:
            own_ref[...] = acc_ref[mine, :features]
            send_ref[...] = acc_ref[other, :features]

    vmem = pl.BlockSpec(memory_space=pltpu.VMEM)
    out = (
        jax.ShapeDtypeStruct(shape, jnp.bfloat16)
        if last
        else jax.ShapeDtypeStruct((tok_rows, features), jnp.float32)
    )
    return pl.pallas_call(
        kernel,
        name="input_grad",
        out_shape=(out, out),
        grid_spec=pltpu.PrefetchScalarGridSpec(
            num_scalar_prefetch=3,
            grid=(),
            in_specs=[vmem] * (2 + len(previous)) + [pl.BlockSpec(memory_space=pl.ANY)] * len(blocks),
            out_specs=(vmem, vmem),
            scratch_shapes=[
                pltpu.VMEM((2 * tok_rows, features + BS), jnp.float32),
                pltpu.VMEM((2 * tok_rows, width), jnp.bfloat16),
                pltpu.VMEM((slots, BS, BS), jnp.bfloat16),
                pltpu.SemaphoreType.DMA((len(copies),)),
            ],
        ),
        compiler_params=pltpu.CompilerParams(vmem_limit_bytes=VMEM_LIMIT),
        cost_estimate=pl.CostEstimate(
            flops=slots * 4 * tok_rows * BS * BS, transcendentals=0, bytes_accessed=12_000_000
        ),
    )(*scalars, own_g, mate_g, *previous, *blocks)


def weight_call(scalars, matrix, capacity, nz, own_g, mate_g, xt, first_run, sizes, run):
    tok_rows = own_g.shape[0]
    width = own_g.shape[1]

    def kernel(lists, place, table, own_g_ref, mate_g_ref, xt_ref, *refs):
        outs, g_ref = refs[:-1], refs[-1]
        known = Lists(lists, place, table, matrix, capacity, run, nz)
        g_ref[tile(place[2]), :] = own_g_ref[...]
        g_ref[tile(1 - place[2]), :] = mate_g_ref[...]
        base = first_run
        for out_ref, runs in zip(outs, sizes):

            def visit(index, carry, out_ref=out_ref, base=base):
                first = known.first(base + index)

                @pl.when(first < known.count)
                def _():
                    for u in range(run):
                        term = jnp.dot(
                            xt_ref[tile(known.row(first + u)), :],
                            g_ref[:, tile(known.col(first + u))],
                            preferred_element_type=jnp.float32,
                        )
                        term = jnp.where(first + u < known.count, term, 0.0)
                        out_ref[index * run + u] = term.astype(out_ref.dtype)

                @pl.when(first >= known.count)
                def _():
                    for u in range(run):
                        out_ref[index * run + u] = jnp.zeros((BS, BS), out_ref.dtype)

                return carry

            lax.fori_loop(0, runs, visit, 0)
            base = base + runs

    vmem = pl.BlockSpec(memory_space=pltpu.VMEM)
    return pl.pallas_call(
        kernel,
        name="weight_grad",
        out_shape=tuple(jax.ShapeDtypeStruct((runs * run, BS, BS), jnp.bfloat16) for runs in sizes),
        grid_spec=pltpu.PrefetchScalarGridSpec(
            num_scalar_prefetch=3,
            grid=(),
            in_specs=[vmem] * 3,
            out_specs=tuple(vmem for _ in sizes),
            scratch_shapes=[pltpu.VMEM((2 * tok_rows, width), jnp.bfloat16)],
        ),
        compiler_params=pltpu.CompilerParams(vmem_limit_bytes=VMEM_LIMIT),
        cost_estimate=pl.CostEstimate(
            flops=sum(sizes) * run * 4 * tok_rows * BS * BS,
            transcendentals=0,
            bytes_accessed=4_000_000 + sum(sizes) * run * 32768,
        ),
    )(*scalars, own_g, mate_g, xt)


def add(*parts):
    total = parts[0].astype(jnp.float32)
    for part in parts[1:]:
        total = total + part.astype(jnp.float32)
    return total.astype(jnp.bfloat16)


def rounds(*values):
    return lax.optimization_barrier(values)


def on_device(
    tokens,
    hidden_grad,
    gate_blocks,
    up_blocks,
    gate_rows,
    gate_cols,
    gate_count,
    up_rows,
    up_cols,
    up_count,
):
    nz, ny = lax.axis_size("z"), lax.axis_size("y")
    side, xl, zid, yid, core = (lax.axis_index(name) for name in AXES)
    half = core ^ (zid % 2)
    home = side == core
    tok_rows = tokens.shape[0]
    run = gate_blocks.shape[1]
    capacity = gate_rows.shape[1]
    width = hidden_grad.shape[1]
    row_blocks = 2 * ny * tokens.shape[1] // BS

    moves = []
    for xh in range(2):
        for z in range(nz):
            for c in range(2):
                moves.append((((c ^ (z % 2)) * nz + z) * 2 + xh, (xh * nz + z) * 2 + c))

    def swap_in(value):
        return lax.ppermute(value, ("xh", "z", "core"), moves)

    def swap_out(value):
        return lax.ppermute(value, ("xh", "z", "core"), [(b, a) for a, b in moves])

    def mate(value):
        return lax.ppermute(value, "core", [(0, 1), (1, 0)])

    def across(value):
        return lax.ppermute(value, "xl", [(0, 1), (1, 0)])

    up_own = swap_in(up_blocks[0])
    up_all = lax.all_gather(up_own, "z", axis=0, tiled=True)
    gate_own = swap_in(gate_blocks[0])
    gate_both = jnp.concatenate([gate_own, across(gate_own)], axis=0)
    packed = jnp.concatenate(
        [gate_rows[0], gate_cols[0], up_rows[0], up_cols[0], gate_count, up_count]
    )
    packed = jnp.where(home, packed, mate(packed))
    other = lax.ppermute(tokens, "xh", [(0, 1), (1, 0)])
    pair = jnp.concatenate(
        [jnp.where(side == 0, tokens, other), jnp.where(side == 0, other, tokens)], axis=0
    )
    from_y = [pair] + [
        lax.ppermute(pair, "y", [(i, (i + s) % ny) for i in range(ny)]) for s in range(1, ny)
    ]
    from_y = jnp.stack(from_y)
    from_y = jnp.stack(
        [lax.dynamic_index_in_dim(from_y, (yid - i) % ny, 0, keepdims=False) for i in range(ny)]
    )
    from_mate = mate(from_y)
    upstream = swap_in(hidden_grad)
    gate_both, up_all, from_mate, upstream, packed = rounds(
        gate_both, up_all, from_mate, upstream, packed
    )
    gate_all = lax.all_gather(gate_both, "z", axis=0, tiled=True)
    up_beside = across(up_all)
    by_core = jnp.stack(
        [jnp.where(core == 0, from_y, from_mate), jnp.where(core == 0, from_mate, from_y)], axis=1
    )
    x = by_core.transpose(2, 0, 1, 3).reshape(2 * tok_rows, row_blocks * BS)
    xt = x.T
    here = jnp.stack([xl, core, half]).astype(jnp.int32)
    gate_scalars = (packed, here, table_of(GATE_RUNS))
    up_scalars = (packed, here, table_of(UP_RUNS))
    part = len(UP_RUNS) // 2 * run
    up_copies = [(0, 0, part, 0), (1, 0, part, part)]

    gate_parts, gate_copies = (gate_all,), [(0, 0, part, 0), (0, part, part, part)]
    up_parts = (up_all, up_beside)

    up_kept, up_sent = forward_call(up_scalars, 1, capacity, nz, x, up_parts, up_copies, width, run)
    up_sent = mate(up_sent)
    gate_kept, gate_sent = forward_call(
        gate_scalars, 0, capacity, nz, x, gate_parts, gate_copies, width, run
    )
    up = up_kept + up_sent
    gate = gate_kept + mate(gate_sent)
    upstream = upstream.astype(jnp.float32)
    sigma = jax.nn.sigmoid(gate)
    activated = gate * sigma
    slope = sigma * (1.0 + gate * (1.0 - sigma))
    gate_grad = (upstream * up * slope).astype(jnp.bfloat16)
    up_grad = (upstream * activated).astype(jnp.bfloat16)
    hidden = (activated * up).astype(jnp.bfloat16)
    gate_mate = mate(gate_grad)
    up_mate = mate(up_grad)

    (gate_terms,) = weight_call(
        gate_scalars, 0, capacity, nz, gate_grad, gate_mate, xt, 0, (len(GATE_RUNS),), run
    )
    gate_sum = lax.psum_scatter(gate_terms, "z", scatter_dimension=0, tiled=True)
    up_mate, gate_terms, hidden = rounds(up_mate, gate_terms, hidden)
    half_runs = len(UP_RUNS) // 2
    up_terms, up_sent = weight_call(
        up_scalars, 1, capacity, nz, up_grad, up_mate, xt, 0, (half_runs, half_runs), run
    )
    up_sent, up_terms, up_mate = rounds(up_sent, up_terms, up_mate)
    up_got = across(up_sent)

    shape = (2, ny, tok_rows, tokens.shape[1])
    shares = input_call(
        up_scalars, 1, capacity, nz, up_grad, up_mate, None, up_parts, up_copies, shape, run
    )
    own, send = input_call(
        gate_scalars, 0, capacity, nz, gate_grad, gate_mate, shares, gate_parts, gate_copies, shape, run
    )
    share = add(own, mate(send))
    kept = lax.dynamic_index_in_dim(share, side, 0, keepdims=False)
    given = lax.dynamic_index_in_dim(share, 1 - side, 0, keepdims=False)
    up_got, given = rounds(up_got, given)
    up_terms = add(up_terms, up_got)
    up_sum = lax.psum_scatter(up_terms, "z", scatter_dimension=0, tiled=True)
    share = add(kept, lax.ppermute(given, "xh", [(0, 1), (1, 0)]))
    total = lax.dynamic_index_in_dim(share, yid, 0, keepdims=False).astype(jnp.float32)
    for step in range(1, ny):
        term = lax.dynamic_index_in_dim(share, (yid + step) % ny, 0, keepdims=False)
        term = lax.ppermute(term, "y", [(i, (i + step) % ny) for i in range(ny)])
        total = total + term.astype(jnp.float32)
    input_grad = swap_out(total.astype(jnp.bfloat16))
    hidden = swap_out(hidden)

    scale = 1.0 / math.sqrt(tok_rows * 4 * nz)
    gate_total = gate_sum[:run].astype(jnp.float32) + across(gate_sum[run:]).astype(jnp.float32)
    gate_out = swap_out((gate_total * scale).astype(jnp.bfloat16))
    up_sum, input_grad, hidden, gate_out = rounds(up_sum, input_grad, hidden, gate_out)
    up_out = swap_out((up_sum.astype(jnp.float32) * scale).astype(jnp.bfloat16))
    return hidden, input_grad, gate_out[None], up_out[None]


def solution(mesh):
    shape = mesh.devices.shape
    fine = Mesh(mesh.devices.reshape(2, 2, shape[0] // 4, shape[1] // 2, 2), AXES)
    seq, hid = ("xh", "xl", "z"), ("y", "core")
    placed = (
        P(seq, hid),
        P(seq, hid),
        P(hid, seq, None, None),
        P(hid, seq, None, None),
        P(hid, None),
        P(hid, None),
        P(hid),
        P(hid, None),
        P(hid, None),
        P(hid),
    )
    return jax.shard_map(
        on_device,
        mesh=fine,
        in_specs=placed,
        out_specs=(P(seq, hid), P(seq, hid), P(hid, seq, None, None), P(hid, seq, None, None)),
        check_vma=False,
    )
```

```python
import math

import jax
import jax.numpy as jnp
import numpy as np
from jax import lax
from jax.experimental import pallas as pl
from jax.experimental.pallas import tpu as pltpu
from jax.sharding import Mesh
from jax.sharding import PartitionSpec as P

AXES = ("xh", "xl", "z", "y", "core")
BS = 128
VMEM_LIMIT = 56 * 1024 * 1024

GATE_RUNS = [(d, r) for d in range(8) for r in (0, 1)]
UP_RUNS = [(d, r) for r in (0, 1) for d in range(8)]
UP_SUMS = [(d, r) for r in (0, 1) for d in (4, 3, -3)] + [(d, r) for r in (0, 1) for d in (2, -2, 1, -1, 0)]
EARLY_RUNS = 8


def tile(index):
    return pl.ds(pl.multiple_of(index * BS, BS), BS)


def start_copies(copies, block_refs, w_ref, sems):
    started = []
    for number, (which, start, size, target) in enumerate(copies):
        copy = pltpu.make_async_copy(
            block_refs[which].at[pl.ds(start, size)], w_ref.at[pl.ds(target, size)], sems.at[number]
        )
        copy.start()
        started.append(copy)
    return started


def over_runs(copies, started, count, run_first, run, body):
    early = EARLY_RUNS * run
    for piece, copy in zip(copies, started):
        if piece[3] < early:
            copy.wait()

    def visit(index, carry):
        first = run_first(index)

        @pl.when(first < count)
        def _():
            body(index, first)

        return carry

    lax.fori_loop(0, EARLY_RUNS, visit, 0)
    for piece, copy in zip(copies, started):
        if piece[3] >= early:
            copy.wait()
    lax.fori_loop(EARLY_RUNS, len(GATE_RUNS), visit, 0)


class Lists:
    def __init__(self, lists, place, table, matrix, capacity, run, nz):
        self.lists, self.place, self.table = lists, place, table
        self.rows, self.cols = 2 * matrix * capacity, (2 * matrix + 1) * capacity
        self.count = lists[4 * capacity + matrix]
        self.capacity, self.run, self.nz = capacity, run, nz

    def first(self, index):
        z = self.table[0, index]
        xl = self.place[0] ^ self.table[1, index]
        return (((self.place[1] ^ (z % 2)) * 2 + xl) * self.nz + z) * self.run

    def row(self, slot):
        return self.lists[self.rows + slot]

    def col(self, slot):
        return self.lists[self.cols + slot]


def table_of(runs):
    return jnp.asarray(np.asarray(runs, np.int32).T)


def forward_call(scalars, matrix, capacity, nz, x, blocks, copies, width, run):
    tok_rows = x.shape[0] // 2
    slots = len(GATE_RUNS) * run

    def kernel(lists, place, table, x_ref, *refs):
        block_refs = refs[: len(blocks)]
        own_ref, send_ref, acc_ref, w_ref, sems = refs[len(blocks) :]
        known = Lists(lists, place, table, matrix, capacity, run, nz)
        started = start_copies(copies, block_refs, w_ref, sems)
        acc_ref[...] = jnp.zeros_like(acc_ref)

        def body(index, first):
            for part in (range(0, 4), range(4, run)):
                products = []
                for u in part:
                    x = x_ref[:, tile(known.row(first + u))]
                    products.append(jnp.dot(x, w_ref[index * run + u], preferred_element_type=jnp.float32))
                for u, product in zip(part, products):
                    col = jnp.where(first + u < known.count, known.col(first + u), width // BS)
                    acc_ref[:, tile(col)] = acc_ref[:, tile(col)] + product

        over_runs(copies, started, known.count, known.first, run, body)
        half = place[2]
        own_ref[...] = acc_ref[tile(half), :width]
        send_ref[...] = acc_ref[tile(1 - half), :width]

    vmem = pl.BlockSpec(memory_space=pltpu.VMEM)
    out = jax.ShapeDtypeStruct((tok_rows, width), jnp.float32)
    return pl.pallas_call(
        kernel,
        name="forward",
        out_shape=(out, out),
        grid_spec=pltpu.PrefetchScalarGridSpec(
            num_scalar_prefetch=3,
            grid=(),
            in_specs=[vmem] + [pl.BlockSpec(memory_space=pl.ANY)] * len(blocks),
            out_specs=(vmem, vmem),
            scratch_shapes=[
                pltpu.VMEM((2 * tok_rows, width + BS), jnp.float32),
                pltpu.VMEM((slots, BS, BS), jnp.bfloat16),
                pltpu.SemaphoreType.DMA((len(copies),)),
            ],
        ),
        compiler_params=pltpu.CompilerParams(vmem_limit_bytes=VMEM_LIMIT),
        cost_estimate=pl.CostEstimate(
            flops=slots * 4 * tok_rows * BS * BS, transcendentals=0, bytes_accessed=8_000_000
        ),
    )(*scalars, x, *blocks)


def input_call(scalars, matrix, capacity, nz, own_g, mate_g, previous, blocks, copies, shape, run):
    tok_rows = own_g.shape[0]
    width = own_g.shape[1]
    features = shape[0] * shape[1] * shape[3]
    slots = len(GATE_RUNS) * run
    last = previous is not None
    previous = previous if last else ()

    def kernel(lists, place, table, own_g_ref, mate_g_ref, *refs):
        before = refs[: len(previous)]
        block_refs = refs[len(previous) : len(previous) + len(blocks)]
        own_ref, send_ref, acc_ref, g_ref, w_ref, sems = refs[len(previous) + len(blocks) :]
        known = Lists(lists, place, table, matrix, capacity, run, nz)
        started = start_copies(copies, block_refs, w_ref, sems)
        mine, other = tile(place[2]), tile(1 - place[2])
        if last:
            acc_ref[mine, :features] = before[0][...]
            acc_ref[other, :features] = before[1][...]
        else:
            acc_ref[...] = jnp.zeros_like(acc_ref)
        g_ref[mine, :] = own_g_ref[...]
        g_ref[other, :] = mate_g_ref[...]

        def body(index, first):
            for part in (range(0, 4), range(4, run)):
                products = []
                for u in part:
                    g = g_ref[:, tile(known.col(first + u))]
                    products.append(
                        lax.dot_general(
                            g,
                            w_ref[index * run + u],
                            (((1,), (1,)), ((), ())),
                            preferred_element_type=jnp.float32,
                        )
                    )
                for u, product in zip(part, products):
                    row = jnp.where(first + u < known.count, known.row(first + u), features // BS)
                    acc_ref[:, tile(row)] = acc_ref[:, tile(row)] + product

        over_runs(copies, started, known.count, known.first, run, body)
        if last:
            step = shape[3]
            for high in range(shape[0]):
                for y in range(shape[1]):
                    cut = pl.ds((y * shape[0] + high) * step, step)
                    own_ref[high, y] = acc_ref[mine, cut].astype(own_ref.dtype)
                    send_ref[high, y] = acc_ref[other, cut].astype(send_ref.dtype)
        else:
            own_ref[...] = acc_ref[mine, :features]
            send_ref[...] = acc_ref[other, :features]

    vmem = pl.BlockSpec(memory_space=pltpu.VMEM)
    out = (
        jax.ShapeDtypeStruct(shape, jnp.bfloat16)
        if last
        else jax.ShapeDtypeStruct((tok_rows, features), jnp.float32)
    )
    return pl.pallas_call(
        kernel,
        name="input_grad",
        out_shape=(out, out),
        grid_spec=pltpu.PrefetchScalarGridSpec(
            num_scalar_prefetch=3,
            grid=(),
            in_specs=[vmem] * (2 + len(previous)) + [pl.BlockSpec(memory_space=pl.ANY)] * len(blocks),
            out_specs=(vmem, vmem),
            scratch_shapes=[
                pltpu.VMEM((2 * tok_rows, features + BS), jnp.float32),
                pltpu.VMEM((2 * tok_rows, width), jnp.bfloat16),
                pltpu.VMEM((slots, BS, BS), jnp.bfloat16),
                pltpu.SemaphoreType.DMA((len(copies),)),
            ],
        ),
        compiler_params=pltpu.CompilerParams(vmem_limit_bytes=VMEM_LIMIT),
        cost_estimate=pl.CostEstimate(
            flops=slots * 4 * tok_rows * BS * BS, transcendentals=0, bytes_accessed=12_000_000
        ),
    )(*scalars, own_g, mate_g, *previous, *blocks)


def weight_call(scalars, matrix, capacity, nz, own_g, mate_g, xt, first_run, sizes, run):
    tok_rows = own_g.shape[0]
    width = own_g.shape[1]

    def kernel(lists, place, table, own_g_ref, mate_g_ref, xt_ref, *refs):
        outs, g_ref = refs[:-1], refs[-1]
        known = Lists(lists, place, table, matrix, capacity, run, nz)
        g_ref[tile(place[2]), :] = own_g_ref[...]
        g_ref[tile(1 - place[2]), :] = mate_g_ref[...]
        base = first_run
        for out_ref, runs in zip(outs, sizes):

            def visit(index, carry, out_ref=out_ref, base=base):
                first = known.first(base + index)

                @pl.when(first < known.count)
                def _():
                    for u in range(run):
                        term = jnp.dot(
                            xt_ref[tile(known.row(first + u)), :],
                            g_ref[:, tile(known.col(first + u))],
                            preferred_element_type=jnp.float32,
                        )
                        term = jnp.where(first + u < known.count, term, 0.0)
                        out_ref[index * run + u] = term.astype(out_ref.dtype)

                @pl.when(first >= known.count)
                def _():
                    for u in range(run):
                        out_ref[index * run + u] = jnp.zeros((BS, BS), out_ref.dtype)

                return carry

            lax.fori_loop(0, runs, visit, 0)
            base = base + runs

    vmem = pl.BlockSpec(memory_space=pltpu.VMEM)
    return pl.pallas_call(
        kernel,
        name="weight_grad",
        out_shape=tuple(jax.ShapeDtypeStruct((runs * run, BS, BS), jnp.bfloat16) for runs in sizes),
        grid_spec=pltpu.PrefetchScalarGridSpec(
            num_scalar_prefetch=3,
            grid=(),
            in_specs=[vmem] * 3,
            out_specs=tuple(vmem for _ in sizes),
            scratch_shapes=[pltpu.VMEM((2 * tok_rows, width), jnp.bfloat16)],
        ),
        compiler_params=pltpu.CompilerParams(vmem_limit_bytes=VMEM_LIMIT),
        cost_estimate=pl.CostEstimate(
            flops=sum(sizes) * run * 4 * tok_rows * BS * BS,
            transcendentals=0,
            bytes_accessed=4_000_000 + sum(sizes) * run * 32768,
        ),
    )(*scalars, own_g, mate_g, xt)


def add(*parts):
    total = parts[0].astype(jnp.float32)
    for part in parts[1:]:
        total = total + part.astype(jnp.float32)
    return total.astype(jnp.bfloat16)


def rounds(*values):
    return lax.optimization_barrier(values)


def on_device(
    tokens,
    hidden_grad,
    gate_blocks,
    up_blocks,
    gate_rows,
    gate_cols,
    gate_count,
    up_rows,
    up_cols,
    up_count,
):
    nz, ny = lax.axis_size("z"), lax.axis_size("y")
    side, xl, zid, yid, core = (lax.axis_index(name) for name in AXES)
    half = core ^ (zid % 2)
    home = side == core
    tok_rows = tokens.shape[0]
    run = gate_blocks.shape[1]
    capacity = gate_rows.shape[1]
    width = hidden_grad.shape[1]
    row_blocks = 2 * ny * tokens.shape[1] // BS

    moves = []
    for xh in range(2):
        for z in range(nz):
            for c in range(2):
                moves.append((((c ^ (z % 2)) * nz + z) * 2 + xh, (xh * nz + z) * 2 + c))

    def swap_in(value):
        return lax.ppermute(value, ("xh", "z", "core"), moves)

    def swap_out(value):
        return lax.ppermute(value, ("xh", "z", "core"), [(b, a) for a, b in moves])

    def mate(value):
        return lax.ppermute(value, "core", [(0, 1), (1, 0)])

    def right(value):
        return lax.ppermute(value, "z", [(i, (i + 1) % nz) for i in range(nz)])

    def left(value):
        return lax.ppermute(value, "z", [(i, (i - 1) % nz) for i in range(nz)])

    def across(value):
        return lax.ppermute(value, "xl", [(0, 1), (1, 0)])

    up_own = swap_in(up_blocks[0])
    up_all = lax.all_gather(up_own, "z", axis=0, tiled=True)
    gate_own = swap_in(gate_blocks[0])
    gate_both = jnp.concatenate([gate_own, across(gate_own)], axis=0)
    packed = jnp.concatenate(
        [gate_rows[0], gate_cols[0], up_rows[0], up_cols[0], gate_count, up_count]
    )
    packed = jnp.where(home, packed, mate(packed))
    other = lax.ppermute(tokens, "xh", [(0, 1), (1, 0)])
    pair = jnp.concatenate(
        [jnp.where(side == 0, tokens, other), jnp.where(side == 0, other, tokens)], axis=0
    )
    from_y = [pair] + [
        lax.ppermute(pair, "y", [(i, (i + s) % ny) for i in range(ny)]) for s in range(1, ny)
    ]
    from_y = jnp.stack(from_y)
    from_y = jnp.stack(
        [lax.dynamic_index_in_dim(from_y, (yid - i) % ny, 0, keepdims=False) for i in range(ny)]
    )
    from_mate = mate(from_y)
    upstream = swap_in(hidden_grad)
    gate_both, up_all, from_mate, upstream, packed = rounds(
        gate_both, up_all, from_mate, upstream, packed
    )
    gate_all = lax.all_gather(gate_both, "z", axis=0, tiled=True)
    up_beside = across(up_all)
    by_core = jnp.stack(
        [jnp.where(core == 0, from_y, from_mate), jnp.where(core == 0, from_mate, from_y)], axis=1
    )
    x = by_core.transpose(2, 0, 1, 3).reshape(2 * tok_rows, row_blocks * BS)
    xt = x.T
    here = jnp.stack([xl, core, half]).astype(jnp.int32)
    gate_scalars = (packed, here, table_of(GATE_RUNS))
    up_scalars = (packed, here, table_of(UP_RUNS))
    part = len(UP_RUNS) // 2 * run
    up_copies = [(0, 0, part, 0), (1, 0, part, part)]

    gate_parts, gate_copies = (gate_all,), [(0, 0, part, 0), (0, part, part, part)]
    up_parts = (up_all, up_beside)

    up_kept, up_sent = forward_call(up_scalars, 1, capacity, nz, x, up_parts, up_copies, width, run)
    up_sent = mate(up_sent)
    gate_kept, gate_sent = forward_call(
        gate_scalars, 0, capacity, nz, x, gate_parts, gate_copies, width, run
    )
    up = up_kept + up_sent
    gate = gate_kept + mate(gate_sent)
    upstream = upstream.astype(jnp.float32)
    sigma = jax.nn.sigmoid(gate)
    activated = gate * sigma
    slope = sigma * (1.0 + gate * (1.0 - sigma))
    gate_grad = (upstream * up * slope).astype(jnp.bfloat16)
    up_grad = (upstream * activated).astype(jnp.bfloat16)
    hidden = (activated * up).astype(jnp.bfloat16)
    gate_mate = mate(gate_grad)
    up_mate = mate(up_grad)

    (gate_terms,) = weight_call(
        gate_scalars, 0, capacity, nz, gate_grad, gate_mate, xt, 0, (len(GATE_RUNS),), run
    )
    gate_sum = lax.psum_scatter(gate_terms, "z", scatter_dimension=0, tiled=True)
    up_mate, gate_terms, hidden = rounds(up_mate, gate_terms, hidden)
    sums = np.asarray(UP_SUMS, np.int32).T
    sum_scalars = (packed, here, jnp.stack([(zid + sums[0] + nz) % nz, jnp.asarray(sums[1])]).astype(jnp.int32))
    u3_kept, u3_sent, u2_kept, u2_sent = weight_call(
        sum_scalars, 1, capacity, nz, up_grad, up_mate, xt, 0, (3, 3, 5, 5), run
    )
    u3_got = across(u3_sent)
    u2_got = across(u2_sent)
    up_mate, u2_kept = rounds(up_mate, u2_kept)
    cut = (run + 1) // 2

    shape = (2, ny, tok_rows, tokens.shape[1])
    shares = input_call(
        up_scalars, 1, capacity, nz, up_grad, up_mate, None, up_parts, up_copies, shape, run
    )
    own, send = input_call(
        gate_scalars, 0, capacity, nz, gate_grad, gate_mate, shares, gate_parts, gate_copies, shape, run
    )
    u3_got, own, send = rounds(u3_got, own, send)
    send = mate(send)
    u3 = add(u3_kept, u3_got)
    r, s = right(u3[:cut]), left(u3[cut:run])
    r, s, send = rounds(r, s, send)
    r = right(jnp.concatenate([add(u3[run : run + cut], r), u3[run + cut : 2 * run]], axis=0))
    s = left(jnp.concatenate([u3[2 * run : 2 * run + cut], add(u3[2 * run + cut :], s)], axis=0))
    share = add(own, send)
    total = lax.dynamic_index_in_dim(share, yid, 1, keepdims=False).astype(jnp.float32)
    for step in range(1, ny):
        term = lax.dynamic_index_in_dim(share, (yid + step) % ny, 1, keepdims=False)
        term = lax.ppermute(term, "y", [(i, (i + step) % ny) for i in range(ny)])
        total = total + term.astype(jnp.float32)
    r, s, u2_got, hidden = rounds(r, s, u2_got, hidden)
    u2 = add(u2_kept, u2_got)
    hidden = swap_out(hidden)
    r, s = right(add(u2[:run], r)), left(add(u2[run : 2 * run], s))
    r, s, total, gate_sum = rounds(r, s, total, gate_sum)
    gate_got = across(gate_sum[run:])
    r, s = right(add(u2[2 * run : 3 * run], r)), left(add(u2[3 * run : 4 * run], s))
    kept = lax.dynamic_index_in_dim(total, side, 0, keepdims=False)
    given = lax.dynamic_index_in_dim(total, 1 - side, 0, keepdims=False).astype(jnp.bfloat16)
    given = lax.ppermute(given, "xh", [(0, 1), (1, 0)])
    r, s, given, gate_got, hidden = rounds(r, s, given, gate_got, hidden)
    input_grad = swap_out((kept + given.astype(jnp.float32)).astype(jnp.bfloat16))
    up_total = u2[4 * run :].astype(jnp.float32) + r.astype(jnp.float32) + s.astype(jnp.float32)

    scale = 1.0 / math.sqrt(tok_rows * 4 * nz)
    gate_total = gate_sum[:run].astype(jnp.float32) + gate_got.astype(jnp.float32)
    both = swap_out((jnp.concatenate([gate_total, up_total], axis=0) * scale).astype(jnp.bfloat16))
    return hidden, input_grad, both[None, :run], both[None, run:]


def solution(mesh):
    shape = mesh.devices.shape
    fine = Mesh(mesh.devices.reshape(2, 2, shape[0] // 4, shape[1] // 2, 2), AXES)
    seq, hid = ("xh", "xl", "z"), ("y", "core")
    placed = (
        P(seq, hid),
        P(seq, hid),
        P(hid, seq, None, None),
        P(hid, seq, None, None),
        P(hid, None),
        P(hid, None),
        P(hid),
        P(hid, None),
        P(hid, None),
        P(hid),
    )
    return jax.shard_map(
        on_device,
        mesh=fine,
        in_specs=placed,
        out_specs=(P(seq, hid), P(seq, hid), P(hid, seq, None, None), P(hid, seq, None, None)),
        check_vma=False,
    )
```

```python
import math

import jax
import jax.numpy as jnp
import numpy as np
from jax import lax
from jax.experimental import pallas as pl
from jax.experimental.pallas import tpu as pltpu
from jax.sharding import Mesh
from jax.sharding import PartitionSpec as P

AXES = ("xh", "xl", "z", "y", "core")
BS = 128
VMEM_LIMIT = 56 * 1024 * 1024

GATE_RUNS = [(d, r) for d in range(8) for r in (0, 1)]
UP_RUNS = [(d, r) for r in (0, 1) for d in range(8)]
UP_SUMS = [(d, r) for r in (0, 1) for d in (4, 3, -3)] + [(d, r) for r in (0, 1) for d in (2, -2, 1, -1, 0)]
EARLY_RUNS = 8


def tile(index):
    return pl.ds(pl.multiple_of(index * BS, BS), BS)


def start_copies(copies, block_refs, w_ref, sems):
    started = []
    for number, (which, start, size, target) in enumerate(copies):
        copy = pltpu.make_async_copy(
            block_refs[which].at[pl.ds(start, size)], w_ref.at[pl.ds(target, size)], sems.at[number]
        )
        copy.start()
        started.append(copy)
    return started


def over_runs(copies, started, count, run_first, run, body):
    early = EARLY_RUNS * run
    for piece, copy in zip(copies, started):
        if piece[3] < early:
            copy.wait()

    def visit(index, carry):
        first = run_first(index)

        @pl.when(first < count)
        def _():
            body(index, first)

        return carry

    lax.fori_loop(0, EARLY_RUNS, visit, 0)
    for piece, copy in zip(copies, started):
        if piece[3] >= early:
            copy.wait()
    lax.fori_loop(EARLY_RUNS, len(GATE_RUNS), visit, 0)


class Lists:
    def __init__(self, lists, place, table, matrix, capacity, run, nz):
        self.lists, self.place, self.table = lists, place, table
        self.rows, self.cols = 2 * matrix * capacity, (2 * matrix + 1) * capacity
        self.count = lists[4 * capacity + matrix]
        self.capacity, self.run, self.nz = capacity, run, nz

    def first(self, index):
        z = self.table[0, index]
        xl = self.place[0] ^ self.table[1, index]
        return (((self.place[1] ^ (z % 2)) * 2 + xl) * self.nz + z) * self.run

    def row(self, slot):
        return self.lists[self.rows + slot]

    def col(self, slot):
        return self.lists[self.cols + slot]


def table_of(runs):
    return jnp.asarray(np.asarray(runs, np.int32).T)


def forward_call(scalars, matrix, capacity, nz, x, blocks, copies, width, run):
    tok_rows = x.shape[0] // 2
    slots = len(GATE_RUNS) * run

    def kernel(lists, place, table, x_ref, *refs):
        block_refs = refs[: len(blocks)]
        own_ref, send_ref, acc_ref, w_ref, sems = refs[len(blocks) :]
        known = Lists(lists, place, table, matrix, capacity, run, nz)
        started = start_copies(copies, block_refs, w_ref, sems)
        acc_ref[...] = jnp.zeros_like(acc_ref)

        def body(index, first):
            for part in (range(0, 4), range(4, run)):
                products = []
                for u in part:
                    x = x_ref[:, tile(known.row(first + u))]
                    products.append(jnp.dot(x, w_ref[index * run + u], preferred_element_type=jnp.float32))
                for u, product in zip(part, products):
                    col = jnp.where(first + u < known.count, known.col(first + u), width // BS)
                    acc_ref[:, tile(col)] = acc_ref[:, tile(col)] + product

        over_runs(copies, started, known.count, known.first, run, body)
        half = place[2]
        own_ref[...] = acc_ref[tile(half), :width]
        send_ref[...] = acc_ref[tile(1 - half), :width]

    vmem = pl.BlockSpec(memory_space=pltpu.VMEM)
    out = jax.ShapeDtypeStruct((tok_rows, width), jnp.float32)
    return pl.pallas_call(
        kernel,
        name="forward",
        out_shape=(out, out),
        grid_spec=pltpu.PrefetchScalarGridSpec(
            num_scalar_prefetch=3,
            grid=(),
            in_specs=[vmem] + [pl.BlockSpec(memory_space=pl.ANY)] * len(blocks),
            out_specs=(vmem, vmem),
            scratch_shapes=[
                pltpu.VMEM((2 * tok_rows, width + BS), jnp.float32),
                pltpu.VMEM((slots, BS, BS), jnp.bfloat16),
                pltpu.SemaphoreType.DMA((len(copies),)),
            ],
        ),
        compiler_params=pltpu.CompilerParams(vmem_limit_bytes=VMEM_LIMIT),
        cost_estimate=pl.CostEstimate(
            flops=slots * 4 * tok_rows * BS * BS, transcendentals=0, bytes_accessed=8_000_000
        ),
    )(*scalars, x, *blocks)


def input_call(scalars, matrix, capacity, nz, own_g, mate_g, previous, blocks, copies, shape, run):
    tok_rows = own_g.shape[0]
    width = own_g.shape[1]
    features = shape[0] * shape[1] * shape[3]
    slots = len(GATE_RUNS) * run
    last = previous is not None
    previous = previous if last else ()

    def kernel(lists, place, table, own_g_ref, mate_g_ref, *refs):
        before = refs[: len(previous)]
        block_refs = refs[len(previous) : len(previous) + len(blocks)]
        own_ref, send_ref, acc_ref, g_ref, w_ref, sems = refs[len(previous) + len(blocks) :]
        known = Lists(lists, place, table, matrix, capacity, run, nz)
        started = start_copies(copies, block_refs, w_ref, sems)
        mine, other = tile(place[2]), tile(1 - place[2])
        if last:
            acc_ref[mine, :features] = before[0][...]
            acc_ref[other, :features] = before[1][...]
        else:
            acc_ref[...] = jnp.zeros_like(acc_ref)
        g_ref[mine, :] = own_g_ref[...]
        g_ref[other, :] = mate_g_ref[...]

        def body(index, first):
            for part in (range(0, 4), range(4, run)):
                products = []
                for u in part:
                    g = g_ref[:, tile(known.col(first + u))]
                    products.append(
                        lax.dot_general(
                            g,
                            w_ref[index * run + u],
                            (((1,), (1,)), ((), ())),
                            preferred_element_type=jnp.float32,
                        )
                    )
                for u, product in zip(part, products):
                    row = jnp.where(first + u < known.count, known.row(first + u), features // BS)
                    acc_ref[:, tile(row)] = acc_ref[:, tile(row)] + product

        over_runs(copies, started, known.count, known.first, run, body)
        if last:
            step = shape[3]
            for high in range(shape[0]):
                for y in range(shape[1]):
                    cut = pl.ds((y * shape[0] + high) * step, step)
                    own_ref[high, y] = acc_ref[mine, cut].astype(own_ref.dtype)
                    send_ref[high, y] = acc_ref[other, cut].astype(send_ref.dtype)
        else:
            own_ref[...] = acc_ref[mine, :features]
            send_ref[...] = acc_ref[other, :features]

    vmem = pl.BlockSpec(memory_space=pltpu.VMEM)
    out = (
        jax.ShapeDtypeStruct(shape, jnp.bfloat16)
        if last
        else jax.ShapeDtypeStruct((tok_rows, features), jnp.float32)
    )
    return pl.pallas_call(
        kernel,
        name="input_grad",
        out_shape=(out, out),
        grid_spec=pltpu.PrefetchScalarGridSpec(
            num_scalar_prefetch=3,
            grid=(),
            in_specs=[vmem] * (2 + len(previous)) + [pl.BlockSpec(memory_space=pl.ANY)] * len(blocks),
            out_specs=(vmem, vmem),
            scratch_shapes=[
                pltpu.VMEM((2 * tok_rows, features + BS), jnp.float32),
                pltpu.VMEM((2 * tok_rows, width), jnp.bfloat16),
                pltpu.VMEM((slots, BS, BS), jnp.bfloat16),
                pltpu.SemaphoreType.DMA((len(copies),)),
            ],
        ),
        compiler_params=pltpu.CompilerParams(vmem_limit_bytes=VMEM_LIMIT),
        cost_estimate=pl.CostEstimate(
            flops=slots * 4 * tok_rows * BS * BS, transcendentals=0, bytes_accessed=12_000_000
        ),
    )(*scalars, own_g, mate_g, *previous, *blocks)


def weight_call(scalars, matrix, capacity, nz, own_g, mate_g, xt, first_run, sizes, run):
    tok_rows = own_g.shape[0]
    width = own_g.shape[1]

    def kernel(lists, place, table, own_g_ref, mate_g_ref, xt_ref, *refs):
        outs, g_ref = refs[:-1], refs[-1]
        known = Lists(lists, place, table, matrix, capacity, run, nz)
        g_ref[tile(place[2]), :] = own_g_ref[...]
        g_ref[tile(1 - place[2]), :] = mate_g_ref[...]
        base = first_run
        for out_ref, runs in zip(outs, sizes):

            def visit(index, carry, out_ref=out_ref, base=base):
                first = known.first(base + index)

                @pl.when(first < known.count)
                def _():
                    for u in range(run):
                        term = jnp.dot(
                            xt_ref[tile(known.row(first + u)), :],
                            g_ref[:, tile(known.col(first + u))],
                            preferred_element_type=jnp.float32,
                        )
                        term = jnp.where(first + u < known.count, term, 0.0)
                        out_ref[index * run + u] = term.astype(out_ref.dtype)

                @pl.when(first >= known.count)
                def _():
                    for u in range(run):
                        out_ref[index * run + u] = jnp.zeros((BS, BS), out_ref.dtype)

                return carry

            lax.fori_loop(0, runs, visit, 0)
            base = base + runs

    vmem = pl.BlockSpec(memory_space=pltpu.VMEM)
    return pl.pallas_call(
        kernel,
        name="weight_grad",
        out_shape=tuple(jax.ShapeDtypeStruct((runs * run, BS, BS), jnp.bfloat16) for runs in sizes),
        grid_spec=pltpu.PrefetchScalarGridSpec(
            num_scalar_prefetch=3,
            grid=(),
            in_specs=[vmem] * 3,
            out_specs=tuple(vmem for _ in sizes),
            scratch_shapes=[pltpu.VMEM((2 * tok_rows, width), jnp.bfloat16)],
        ),
        compiler_params=pltpu.CompilerParams(vmem_limit_bytes=VMEM_LIMIT),
        cost_estimate=pl.CostEstimate(
            flops=sum(sizes) * run * 4 * tok_rows * BS * BS,
            transcendentals=0,
            bytes_accessed=4_000_000 + sum(sizes) * run * 32768,
        ),
    )(*scalars, own_g, mate_g, xt)


def add(*parts):
    total = parts[0].astype(jnp.float32)
    for part in parts[1:]:
        total = total + part.astype(jnp.float32)
    return total.astype(jnp.bfloat16)


def rounds(*values):
    return lax.optimization_barrier(values)


def on_device(
    tokens,
    hidden_grad,
    gate_blocks,
    up_blocks,
    gate_rows,
    gate_cols,
    gate_count,
    up_rows,
    up_cols,
    up_count,
):
    nz, ny = lax.axis_size("z"), lax.axis_size("y")
    side, xl, zid, yid, core = (lax.axis_index(name) for name in AXES)
    half = core ^ (zid % 2)
    home = side == core
    tok_rows = tokens.shape[0]
    run = gate_blocks.shape[1]
    capacity = gate_rows.shape[1]
    width = hidden_grad.shape[1]
    row_blocks = 2 * ny * tokens.shape[1] // BS

    moves = []
    for xh in range(2):
        for z in range(nz):
            for c in range(2):
                moves.append((((c ^ (z % 2)) * nz + z) * 2 + xh, (xh * nz + z) * 2 + c))

    def swap_in(value):
        return lax.ppermute(value, ("xh", "z", "core"), moves)

    def swap_out(value):
        return lax.ppermute(value, ("xh", "z", "core"), [(b, a) for a, b in moves])

    def mate(value):
        return lax.ppermute(value, "core", [(0, 1), (1, 0)])

    def right(value):
        return lax.ppermute(value, "z", [(i, (i + 1) % nz) for i in range(nz)])

    def left(value):
        return lax.ppermute(value, "z", [(i, (i - 1) % nz) for i in range(nz)])

    def across(value):
        return lax.ppermute(value, "xl", [(0, 1), (1, 0)])

    up_own = swap_in(up_blocks[0])
    up_all = lax.all_gather(up_own, "z", axis=0, tiled=True)
    gate_own = swap_in(gate_blocks[0])
    gate_both = jnp.concatenate([gate_own, across(gate_own)], axis=0)
    packed = jnp.concatenate(
        [gate_rows[0], gate_cols[0], up_rows[0], up_cols[0], gate_count, up_count]
    )
    packed = jnp.where(home, packed, mate(packed))
    other = lax.ppermute(tokens, "xh", [(0, 1), (1, 0)])
    pair = jnp.concatenate(
        [jnp.where(side == 0, tokens, other), jnp.where(side == 0, other, tokens)], axis=0
    )
    from_y = [pair] + [
        lax.ppermute(pair, "y", [(i, (i + s) % ny) for i in range(ny)]) for s in range(1, ny)
    ]
    from_y = jnp.stack(from_y)
    from_y = jnp.stack(
        [lax.dynamic_index_in_dim(from_y, (yid - i) % ny, 0, keepdims=False) for i in range(ny)]
    )
    from_mate = mate(from_y)
    upstream = swap_in(hidden_grad)
    gate_both, up_all, from_mate, upstream, packed = rounds(
        gate_both, up_all, from_mate, upstream, packed
    )
    gate_all = lax.all_gather(gate_both, "z", axis=0, tiled=True)
    up_beside = across(up_all)
    by_core = jnp.stack(
        [jnp.where(core == 0, from_y, from_mate), jnp.where(core == 0, from_mate, from_y)], axis=1
    )
    x = by_core.transpose(2, 0, 1, 3).reshape(2 * tok_rows, row_blocks * BS)
    xt = x.T
    here = jnp.stack([xl, core, half]).astype(jnp.int32)
    gate_scalars = (packed, here, table_of(GATE_RUNS))
    up_scalars = (packed, here, table_of(UP_RUNS))
    part = len(UP_RUNS) // 2 * run
    up_copies = [(0, 0, part, 0), (1, 0, part, part)]

    gate_parts, gate_copies = (gate_all,), [(0, 0, part, 0), (0, part, part, part)]
    up_parts = (up_all, up_beside)

    up_kept, up_sent = forward_call(up_scalars, 1, capacity, nz, x, up_parts, up_copies, width, run)
    up_sent = mate(up_sent)
    gate_kept, gate_sent = forward_call(
        gate_scalars, 0, capacity, nz, x, gate_parts, gate_copies, width, run
    )
    up = up_kept + up_sent
    gate = gate_kept + mate(gate_sent)
    upstream = upstream.astype(jnp.float32)
    sigma = jax.nn.sigmoid(gate)
    activated = gate * sigma
    slope = sigma * (1.0 + gate * (1.0 - sigma))
    gate_grad = (upstream * up * slope).astype(jnp.bfloat16)
    up_grad = (upstream * activated).astype(jnp.bfloat16)
    hidden = (activated * up).astype(jnp.bfloat16)
    gate_mate = mate(gate_grad)
    up_mate = mate(up_grad)

    (gate_terms,) = weight_call(
        gate_scalars, 0, capacity, nz, gate_grad, gate_mate, xt, 0, (len(GATE_RUNS),), run
    )
    gate_sum = lax.psum_scatter(gate_terms, "z", scatter_dimension=0, tiled=True)
    up_mate, gate_terms, hidden = rounds(up_mate, gate_terms, hidden)
    sums = np.asarray(UP_SUMS, np.int32).T
    sum_scalars = (packed, here, jnp.stack([(zid + sums[0] + nz) % nz, jnp.asarray(sums[1])]).astype(jnp.int32))
    u3_kept, u3_sent, u2_kept, u1_kept, u2_sent, u1_sent = weight_call(
        sum_scalars, 1, capacity, nz, up_grad, up_mate, xt, 0, (3, 3, 2, 3, 2, 3), run
    )
    u3_got = across(u3_sent)
    u2_got = across(u2_sent)
    u1_got = across(u1_sent)
    up_mate, u2_kept = rounds(up_mate, u2_kept)
    cut = (run + 1) // 2

    shape = (2, ny, tok_rows, tokens.shape[1])
    shares = input_call(
        up_scalars, 1, capacity, nz, up_grad, up_mate, None, up_parts, up_copies, shape, run
    )
    *shares, u3_got = rounds(*shares, u3_got)
    u3 = add(u3_kept, u3_got)
    r, s = right(u3[:cut]), left(u3[cut:run])
    own, send = input_call(
        gate_scalars, 0, capacity, nz, gate_grad, gate_mate, tuple(shares), gate_parts, gate_copies, shape, run
    )
    send = mate(send)
    r, s, send = rounds(r, s, send)
    r = right(jnp.concatenate([add(u3[run : run + cut], r), u3[run + cut : 2 * run]], axis=0))
    s = left(jnp.concatenate([u3[2 * run : 2 * run + cut], add(u3[2 * run + cut :], s)], axis=0))
    share = add(own, send)
    total = lax.dynamic_index_in_dim(share, yid, 1, keepdims=False).astype(jnp.float32)
    for step in range(1, ny):
        term = lax.dynamic_index_in_dim(share, (yid + step) % ny, 1, keepdims=False)
        term = lax.ppermute(term, "y", [(i, (i + step) % ny) for i in range(ny)])
        total = total + term.astype(jnp.float32)
    r, s, u2_got, hidden = rounds(r, s, u2_got, hidden)
    u2 = add(u2_kept, u2_got)
    hidden = swap_out(hidden)
    r, s = right(add(u2[:run], r)), left(add(u2[run : 2 * run], s))
    r, s, total, gate_sum, u1_got = rounds(r, s, total, gate_sum, u1_got)
    u1 = add(u1_kept, u1_got)
    gate_got = across(gate_sum[run:])
    r, s = right(add(u1[:run], r)), left(add(u1[run : 2 * run], s))
    kept = lax.dynamic_index_in_dim(total, side, 0, keepdims=False)
    given = lax.dynamic_index_in_dim(total, 1 - side, 0, keepdims=False).astype(jnp.bfloat16)
    given = lax.ppermute(given, "xh", [(0, 1), (1, 0)])
    r, s, given, gate_got, hidden = rounds(r, s, given, gate_got, hidden)
    input_grad = swap_out((kept + given.astype(jnp.float32)).astype(jnp.bfloat16))
    up_total = u1[2 * run :].astype(jnp.float32) + r.astype(jnp.float32) + s.astype(jnp.float32)

    scale = 1.0 / math.sqrt(tok_rows * 4 * nz)
    gate_total = gate_sum[:run].astype(jnp.float32) + gate_got.astype(jnp.float32)
    both = swap_out((jnp.concatenate([gate_total, up_total], axis=0) * scale).astype(jnp.bfloat16))
    return hidden, input_grad, both[None, :run], both[None, run:]


def solution(mesh):
    shape = mesh.devices.shape
    fine = Mesh(mesh.devices.reshape(2, 2, shape[0] // 4, shape[1] // 2, 2), AXES)
    seq, hid = ("xh", "xl", "z"), ("y", "core")
    placed = (
        P(seq, hid),
        P(seq, hid),
        P(hid, seq, None, None),
        P(hid, seq, None, None),
        P(hid, None),
        P(hid, None),
        P(hid),
        P(hid, None),
        P(hid, None),
        P(hid),
    )
    return jax.shard_map(
        on_device,
        mesh=fine,
        in_specs=placed,
        out_specs=(P(seq, hid), P(seq, hid), P(hid, seq, None, None), P(hid, seq, None, None)),
        check_vma=False,
    )
```
